32 devices in a mesh: seq: 16 (over z, x, core), tp: 2 (over y).
Axes of the slice: x: 2, y: 2, z: 4, core: 2. Of those that a mesh axis runs over, the one named last changes fastest.
Arguments:
- states: bfloat16 [4096, 4096], P('seq', 'tp'), may hold values from -1.5 to 1.5
- doc_lengths: int32 [4], replicated, may hold values from 1 to 2048, 4096 in all
- attn_gain: float32 [4096], replicated, may hold values from 0.9 to 6
- query_weight: bfloat16 [4096, 4096], P(None, 'tp'), may hold values from -0.09375 to 0.09375
- key_weight: bfloat16 [4096, 1024], P(None, 'tp'), may hold values from -0.09375 to 0.09375
- value_weight: bfloat16 [4096, 1024], P(None, 'tp'), may hold values from -0.09375 to 0.09375
- output_weight: bfloat16 [4096, 4096], P('tp'), may hold values from -0.5 to 0.5
- mlp_gain: float32 [4096], replicated, may hold values from 0.5 to 1.5
- gate_weight: bfloat16 [4096, 7168], P('seq', 'tp'), may hold values from -0.09375 to 0.09375
- up_weight: bfloat16 [4096, 7168], P('seq', 'tp'), may hold values from -0.09375 to 0.09375
- down_weight: bfloat16 [7168, 4096], P('tp', 'seq'), may hold values from -0.0625 to 0.0625
Outputs:
- layer_out: bfloat16 [4096, 4096], P('seq', 'tp')
The draws below stay inside these ranges and needn't reach their ends.
Inputs may be any that keep to these rules, and one draw needn't show every extreme that they name: `doc_lengths`: 4 documents that fill the 4096 tokens in order.
All inputs are finite; a program needn't handle non-finite values.
Results may differ from the reference program's by a relative error of at most 0.014.
The reference program's roundings to bfloat16 on the way count: a program that leaves them out, or rounds other values in their place, can miss the bound.
Values may be sent and summed in bfloat16 or wider, within the bound.
No kernel may reach another device: no remote copies, remote signals or barrier semaphores. Data moves between devices by JAX's collectives and lax.ppermute only.
A program may use at most 192 MiB of HBM per device.

```python
import math
import jax
import jax.numpy as jnp
import numpy as np
from jax import lax

D = 4096
HEADS = 32
KV_HEADS = 8
HD = 128
FF = 7168
SEQS = 4
TOKENS = 4096


def draw_attn_gain(key, part):
    return jax.random.uniform(key, (D,), jnp.float32, 0.9, 1.1)


def block_scale(key, extent, split, smallest, high):
    loudness = 1.0
    for axis_at, blocks in split:
        heights = jax.random.uniform(jax.random.fold_in(jax.random.fold_in(key, 6), axis_at), (blocks,), jnp.float32, smallest / len(split), high / len(split))
        loudness = loudness * jnp.repeat(jnp.exp(heights), extent[axis_at] // blocks).reshape((-1,) + (1,) * (len(extent) - 1 - axis_at))
    return loudness


def profile(amount, total, most, skew):
    portions = [(1 << 20) // math.isqrt(standing ** skew) + 1 for standing in range(2, amount + 1)]
    rest, holding = total - most - (amount - 1), [1] * (amount - 1)
    while rest > 0:
        candidates = [i for i in range(amount - 1) if holding[i] < most]
        mass, remaining = sum([portions[i] for i in candidates]), rest
        for i in candidates:
            extra = min(most - holding[i], max(1, remaining * portions[i] // mass), rest)
            holding[i] = holding[i] + extra
            rest = rest - extra
    return np.array([most] + holding)


def ragged(own_key, count, total, bound, skew):
    if count == 2:
        one = jax.random.randint(own_key, (), max(1, total - bound), min(bound, total - 1) + 1)
        return jnp.stack([one, total - one])
    tallies = jnp.asarray(profile(count, total, bound, skew), jnp.int32)
    twos = (count - 1) // 2
    source_of, receiver = tallies[1:1 + 2 * twos:2], tallies[2:2 + 2 * twos:2]
    room = jnp.minimum(source_of - 1, bound - receiver)
    moved = jax.random.randint(jax.random.fold_in(own_key, 1), (twos,), 0, 1 << 20) % (room + 1)
    tallies = tallies.at[1:1 + 2 * twos:2].set(source_of - moved).at[2:2 + 2 * twos:2].set(receiver + moved)
    return tallies[jax.random.permutation(jax.random.fold_in(own_key, 2), count)]


def gaussian(stream_key, dims, scale, limit, split=(), dtype=jnp.bfloat16):
    array = jax.random.normal(stream_key, dims, jnp.float32) * scale
    if len(split) > 0:
        array = block_scale(stream_key, dims, split, -0.22, 0.18) * array
    return jnp.clip(array, min=-limit, max=limit).astype(dtype)


def setup_inputs(seed: int = 0) -> dict:
    splits = jax.random.split(jax.random.key(seed), 12)
    states = gaussian(splits[0], (TOKENS, D), 0.1, 1.5, ((0, 16), (1, 2)))
    doc_lengths = ragged(splits[1], SEQS, TOKENS, TOKENS // 2, 2).astype(jnp.int32)
    attn_gain = draw_attn_gain(jax.random.fold_in(splits[11], 71), 0)
    query_weight = gaussian(splits[3], (D, HEADS * HD), D ** -0.5, 0.09375, ((1, 2),))
    key_weight = gaussian(splits[4], (D, KV_HEADS * HD), D ** -0.5, 0.09375, ((1, 2),))
    value_weight = gaussian(splits[5], (D, KV_HEADS * HD), D ** -0.5, 0.09375, ((1, 2),))
    output_weight = gaussian(splits[6], (HEADS * HD, D), HD ** -0.5, 0.5, ((0, 2),))
    mlp_gain = jnp.clip(1.0 + 0.1 * jax.random.normal(splits[7], (D,), jnp.float32), 0.5, 1.5)
    gate_weight = gaussian(splits[8], (D, FF), D ** -0.5, 0.09375, ((0, 16), (1, 2)))
    up_weight = gaussian(splits[9], (D, FF), D ** -0.5, 0.09375, ((0, 16), (1, 2)))
    down_weight = gaussian(splits[10], (FF, D), FF ** -0.5, 0.0625, ((0, 2), (1, 16)))
    return dict(states=states, doc_lengths=doc_lengths, attn_gain=attn_gain, query_weight=query_weight, key_weight=key_weight, value_weight=value_weight, output_weight=output_weight, mlp_gain=mlp_gain, gate_weight=gate_weight, up_weight=up_weight, down_weight=down_weight)


EPS = 1e-05
THETA = 500000.0

def rms_norm(rows, gain):
    rows = rows.astype(jnp.float32)
    factor = lax.rsqrt(lax.optimization_barrier(jnp.mean(rows * rows, axis=-1, keepdims=True)) + EPS)
    return (rows * factor * gain.astype(jnp.float32)).astype(jnp.bfloat16)

def rotary(block, where):
    half = block.shape[-1] // 2
    freq = THETA ** (-2.0 * jnp.arange(half).astype(jnp.float32) / block.shape[-1])
    angle = where.astype(jnp.float32)[:, None] * freq[None, :]
    cosine = jnp.cos(angle)[:, None, :]
    sine = jnp.sin(angle)[:, None, :]
    first = block[..., :half]
    second = block[..., half:]
    return jnp.concatenate([first * cosine - second * sine, second * cosine + first * sine], axis=-1)

def doc_layout(spots, lengths):
    ends = jnp.cumsum(lengths).astype(jnp.int32)
    after = spots[:, None] >= ends[None, :]
    documents = lax.optimization_barrier(jnp.sum(after.astype(jnp.int32), axis=1)).astype(jnp.int32)
    begins = lax.optimization_barrier(jnp.sum(jnp.where(after, lengths[None, :], 0), axis=1)).astype(jnp.int32)
    return (documents, (spots - begins).astype(jnp.int32))

def reference(states, doc_lengths, attn_gain, query_weight, key_weight, value_weight, output_weight, mlp_gain, gate_weight, up_weight, down_weight):
    tokens = states.shape[0]
    spots = jnp.arange(tokens).astype(jnp.int32)
    documents, where = doc_layout(spots, doc_lengths)
    normed = rms_norm(states, attn_gain)
    query = jnp.dot(normed, query_weight, preferred_element_type=jnp.float32).reshape(tokens, HEADS, HD)
    query = rotary(query, where).astype(jnp.bfloat16)
    keys = jnp.dot(normed, key_weight, preferred_element_type=jnp.float32).reshape(tokens, KV_HEADS, HD)
    keys = rotary(keys, where).astype(jnp.bfloat16)
    values = jnp.dot(normed, value_weight, preferred_element_type=jnp.float32).astype(jnp.bfloat16).reshape(tokens, KV_HEADS, HD)
    allowed = (documents[:, None] == documents[None, :]) & (spots[None, :] <= spots[:, None])
    group = HEADS // KV_HEADS
    scale = HD ** (-0.5)

    def one_head(head):
        q_head = lax.dynamic_index_in_dim(query, head, 1, keepdims=False)
        k_head = lax.dynamic_index_in_dim(keys, head // group, 1, keepdims=False)
        v_head = lax.dynamic_index_in_dim(values, head // group, 1, keepdims=False)
        scores = jnp.dot(q_head, k_head.T, preferred_element_type=jnp.float32) * scale
        masked = jnp.where(allowed, scores, -1e+30)
        highest = lax.optimization_barrier(jnp.max(masked, axis=1, keepdims=True))
        weights = jnp.where(allowed, jnp.exp(masked - highest), 0.0)
        total = lax.optimization_barrier(jnp.sum(weights, axis=1, keepdims=True))
        summed = jnp.dot(weights.astype(jnp.bfloat16), v_head, preferred_element_type=jnp.float32)
        return (summed / total).astype(jnp.bfloat16)
    heads_out = lax.map(one_head, jnp.arange(HEADS).astype(jnp.int32))
    attended = jnp.transpose(heads_out, (1, 0, 2)).reshape(tokens, HEADS * HD)
    mixed = (states.astype(jnp.float32) + jnp.dot(attended, output_weight, preferred_element_type=jnp.float32)).astype(jnp.bfloat16)
    normed_mlp = rms_norm(mixed, mlp_gain)
    gate = jnp.dot(normed_mlp, gate_weight, preferred_element_type=jnp.float32)
    up = jnp.dot(normed_mlp, up_weight, preferred_element_type=jnp.float32)
    hidden = (jax.nn.silu(gate) * up).astype(jnp.bfloat16)
    return (mixed.astype(jnp.float32) + jnp.dot(hidden, down_weight, preferred_element_type=jnp.float32)).astype(jnp.bfloat16)
```

```python
import functools
import math

import jax
import jax.numpy as jnp
from jax import lax
from jax.experimental import pallas as pl
from jax.experimental.pallas import tpu as pltpu
from jax.sharding import PartitionSpec as P

HD = 128


EPS = 1e-05
THETA = 500000.0
SWAP = [(0, 1), (1, 0)]


def rms_norm(rows, gain):
    rows = rows.astype(jnp.float32)
    factor = lax.rsqrt(jnp.mean(rows * rows, axis=-1, keepdims=True) + EPS)
    return (rows * factor * gain).astype(jnp.bfloat16)


def rotary(block, where):
    half = block.shape[-1] // 2
    freq = THETA ** (-2.0 * jnp.arange(half).astype(jnp.float32) / block.shape[-1])
    angle = where.astype(jnp.float32)[:, None] * freq[None, :]
    cosine = jnp.cos(angle)[:, None, :]
    sine = jnp.sin(angle)[:, None, :]
    first = block[..., :half]
    second = block[..., half:]
    return jnp.concatenate(
        [first * cosine - second * sine, second * cosine + first * sine], axis=-1
    )


def norm_pair_kernel(place_ref, own_ref, other_ref, gain_ref, out_ref):
    width = own_ref.shape[1]
    own = own_ref[...].astype(jnp.float32)
    other = other_ref[...].astype(jnp.float32)
    square = jnp.sum(own * own, axis=-1, keepdims=True) + jnp.sum(
        other * other, axis=-1, keepdims=True
    )
    factor = lax.rsqrt(square / (2 * width) + EPS)
    at_own = pl.multiple_of(place_ref[0] * width, width)
    at_other = pl.multiple_of((1 - place_ref[0]) * width, width)
    gain_own = gain_ref[:, pl.ds(at_own, width)]
    gain_other = gain_ref[:, pl.ds(at_other, width)]
    out_ref[:, pl.ds(at_own, width)] = (own * factor * gain_own).astype(out_ref.dtype)
    out_ref[:, pl.ds(at_other, width)] = (other * factor * gain_other).astype(out_ref.dtype)


def norm_pair(own, other, gain, place):
    rows, width = own.shape
    tile = 64 if rows % 64 == 0 else rows
    return pl.pallas_call(
        norm_pair_kernel,
        out_shape=jax.ShapeDtypeStruct((rows, 2 * width), own.dtype),
        grid_spec=pltpu.PrefetchScalarGridSpec(
            num_scalar_prefetch=1,
            grid=(rows // tile,),
            in_specs=[
                pl.BlockSpec((tile, width), lambda i, p: (i, 0)),
                pl.BlockSpec((tile, width), lambda i, p: (i, 0)),
                pl.BlockSpec((1, 2 * width), lambda i, p: (0, 0)),
            ],
            out_specs=pl.BlockSpec((tile, 2 * width), lambda i, p: (i, 0)),
        ),
        name="norm_pair",
    )(place.reshape(1), own, other, gain.reshape(1, -1))


def attend_kernel(
    group, info_ref, q_ref, k_ref, v_ref, start_ref, out_ref, heads, scores, high, total, summed
):
    rows = q_ref.shape[0]
    head_dim = k_ref.shape[1]
    coefficient = head_dim ** (-0.5) * math.log2(math.e)
    lowest, own, plain = info_ref[0], info_ref[1], info_ref[2]
    for member in range(group):
        heads[member * rows : (member + 1) * rows, :] = q_ref[
            :, member * head_dim : (member + 1) * head_dim
        ]
    high[...] = jnp.full_like(high, -1e30)
    total[...] = jnp.zeros_like(total)
    summed[...] = jnp.zeros_like(summed)

    def score(block, masked):
        at = pl.multiple_of(block * rows, rows)
        keys = k_ref[pl.ds(at, rows), :]
        if masked:
            spot = at + lax.broadcasted_iota(jnp.int32, (rows, rows), 1)
            query = own * rows + lax.broadcasted_iota(jnp.int32, (rows, rows), 0)
            allowed = (spot >= start_ref[...]) & (spot <= query)
        for member in range(group):
            part = pl.ds(member * rows, rows)
            value = lax.dot_general(
                heads[part, :], keys, (((1,), (1,)), ((), ())), preferred_element_type=jnp.float32
            )
            if masked:
                value = jnp.where(allowed, value, -1e30)
            scores[block, part, :] = value
            high[part, :] = jnp.maximum(high[part, :], value)

    def first(block, carry):
        clear = (block >= plain) & (block < own)

        @pl.when(clear)
        def _():
            score(block, False)

        @pl.when(jnp.logical_not(clear))
        def _():
            score(block, True)

        return carry

    lax.fori_loop(lowest, own + 1, first, 0)
    for member in range(group):
        part = pl.ds(member * rows, rows)
        high[part, :] = jnp.broadcast_to(
            jnp.max(high[part, :], axis=-1, keepdims=True), (rows, rows)
        )

    def second(block, carry):
        at = pl.multiple_of(block * rows, rows)
        values = v_ref[pl.ds(at, rows), :]
        for member in range(group):
            part = pl.ds(member * rows, rows)
            weight = jnp.exp2((scores[block, part, :] - high[part, :]) * coefficient)
            total[part, :] = total[part, :] + weight
            summed[part, :] = summed[part, :] + jnp.dot(
                weight.astype(values.dtype), values, preferred_element_type=jnp.float32
            )
        return carry

    lax.fori_loop(lowest, own + 1, second, 0)
    for member in range(group):
        part = pl.ds(member * rows, rows)
        whole = jnp.sum(total[part, :], axis=-1, keepdims=True)
        out_ref[:, member * head_dim : (member + 1) * head_dim] = (
            summed[part, :] / whole
        ).astype(out_ref.dtype)


def attend(query, both, start, info, kv_local, group):
    rows = query.shape[0]
    count = both.shape[0]
    return pl.pallas_call(
        functools.partial(attend_kernel, group),
        out_shape=jax.ShapeDtypeStruct(query.shape, query.dtype),
        grid_spec=pltpu.PrefetchScalarGridSpec(
            num_scalar_prefetch=1,
            grid=(kv_local,),
            in_specs=[
                pl.BlockSpec((rows, group * HD), lambda g, i: (0, g)),
                pl.BlockSpec((count, HD), lambda g, i: (0, g)),
                pl.BlockSpec((count, HD), lambda g, i: (0, kv_local + g)),
                pl.BlockSpec((rows, 1), lambda g, i: (0, 0)),
            ],
            out_specs=pl.BlockSpec((rows, group * HD), lambda g, i: (0, g)),
            scratch_shapes=[
                pltpu.VMEM((group * rows, HD), query.dtype),
                pltpu.VMEM((count // rows, group * rows, rows), jnp.float32),
                pltpu.VMEM((group * rows, rows), jnp.float32),
                pltpu.VMEM((group * rows, rows), jnp.float32),
                pltpu.VMEM((group * rows, HD), jnp.float32),
            ],
        ),
        name="attend",
    )(info, query, both, both, start)


def hidden_kernel(half_ref, a_ref, b_ref, ga_ref, ua_ref, gb_ref, ub_ref, out_ref):
    a = a_ref[...]
    b = b_ref[...]
    gate = jnp.dot(a, ga_ref[...], preferred_element_type=jnp.float32) + jnp.dot(
        b, gb_ref[...], preferred_element_type=jnp.float32
    )
    up = jnp.dot(a, ua_ref[...], preferred_element_type=jnp.float32) + jnp.dot(
        b, ub_ref[...], preferred_element_type=jnp.float32
    )
    out_ref[...] = (gate / (1.0 + jnp.exp(-gate)) * up).astype(out_ref.dtype)


def hidden_of(normed, near, far, half):
    rows, width = normed.shape
    units = near.shape[1] // 2
    if units % 256:
        joined = jnp.where(
            half == 0, jnp.concatenate([near, far]), jnp.concatenate([far, near])
        )
        both = jnp.dot(normed, joined, preferred_element_type=jnp.float32)
        return (jax.nn.silu(both[:, :units]) * both[:, units:]).astype(normed.dtype)
    tile = 256
    steps = units // tile
    return pl.pallas_call(
        hidden_kernel,
        out_shape=jax.ShapeDtypeStruct((rows, units), normed.dtype),
        grid_spec=pltpu.PrefetchScalarGridSpec(
            num_scalar_prefetch=1,
            grid=(steps,),
            in_specs=[
                pl.BlockSpec((rows, width // 2), lambda n, h: (0, h[0])),
                pl.BlockSpec((rows, width // 2), lambda n, h: (0, 1 - h[0])),
                pl.BlockSpec((width // 2, tile), lambda n, h: (0, n)),
                pl.BlockSpec((width // 2, tile), lambda n, h: (0, steps + n)),
                pl.BlockSpec((width // 2, tile), lambda n, h: (0, n)),
                pl.BlockSpec((width // 2, tile), lambda n, h: (0, steps + n)),
            ],
            out_specs=pl.BlockSpec((rows, tile), lambda n, h: (0, n)),
        ),
        name="hidden",
    )(half.reshape(1), normed, normed, near, near, far, far)


def per_device(
    states,
    doc_lengths,
    attn_gain,
    query_weight,
    key_weight,
    value_weight,
    output_weight,
    mlp_gain,
    gate_weight,
    up_weight,
    down_weight,
):
    tok_rows, own_width = states.shape
    head_dim = HD
    kv_local = key_weight.shape[1] // head_dim
    q_local = query_weight.shape[1] // head_dim
    group = q_local // kv_local
    spots = lax.axis_size("seq")
    ranks = lax.axis_size("tp")
    spot = lax.axis_index("seq")
    rank = lax.axis_index("tp")
    side = spots // 2
    half = spot // side
    across = [(i, (i + side) % spots) for i in range(spots)]
    halves = [list(range(side)), list(range(side, spots))]
    units = gate_weight.shape[1] // 2

    def part(array, index, size, axis):
        return lax.dynamic_slice_in_dim(array, index * size, size, axis)

    def norm_full(own, gain):
        if ranks == 2:
            return norm_pair(own, lax.ppermute(own, "tp", SWAP), gain, rank)
        return rms_norm(lax.all_gather(own, "tp", axis=1, tiled=True), gain)

    def gather_half(array, axis):
        return lax.all_gather(
            array, "seq", axis=axis, tiled=True, axis_index_groups=halves
        )

    near = jnp.concatenate(
        [part(gate_weight, half, units, 1), part(up_weight, half, units, 1)], axis=1
    )
    far = jnp.concatenate(
        [part(gate_weight, 1 - half, units, 1), part(up_weight, 1 - half, units, 1)], axis=1
    )
    far = lax.ppermute(far, "seq", across)
    down_near = part(down_weight, half, units, 0)
    down_far = lax.ppermute(part(down_weight, 1 - half, units, 0), "seq", across)

    ends = jnp.cumsum(doc_lengths)
    own_rows = spot * tok_rows + jnp.arange(tok_rows)
    after = own_rows[:, None] >= ends[None, :]
    start = jnp.sum(jnp.where(after, doc_lengths[None, :], 0), axis=1)
    where = own_rows - start

    normed = norm_full(states, attn_gain)
    keys = jnp.dot(normed, key_weight, preferred_element_type=jnp.float32).reshape(
        tok_rows, kv_local, head_dim
    )
    keys = rotary(keys, where).astype(jnp.bfloat16).reshape(tok_rows, kv_local * head_dim)
    values = jnp.dot(normed, value_weight, preferred_element_type=jnp.float32).astype(jnp.bfloat16)
    both = lax.all_gather(
        jnp.concatenate([keys, values], axis=1), "seq", axis=0, tiled=True
    )
    query = jnp.dot(normed, query_weight, preferred_element_type=jnp.float32).reshape(
        tok_rows, q_local, head_dim
    )
    query = rotary(query, where).astype(jnp.bfloat16).reshape(tok_rows, q_local * head_dim)
    info = jnp.stack(
        [start[0] // tok_rows, spot, (start[-1] + tok_rows - 1) // tok_rows]
    ).astype(jnp.int32)
    attended = attend(
        query, both, start.astype(jnp.int32).reshape(tok_rows, 1), info, kv_local, group
    )

    partial_value = jnp.dot(attended, output_weight, preferred_element_type=jnp.float32)
    if ranks == 2:
        sent = part(partial_value, 1 - rank, own_width, 1).astype(jnp.bfloat16)
        got = lax.ppermute(sent, "tp", SWAP)
        shares = part(partial_value, rank, own_width, 1) + got.astype(jnp.float32)
    else:
        shares = lax.psum_scatter(partial_value, "tp", scatter_dimension=1, tiled=True)
    mixed = (states.astype(jnp.float32) + shares).astype(jnp.bfloat16)

    mixed_far = lax.ppermute(mixed, "seq", across)
    normed_mlp = jnp.concatenate(
        [norm_full(mixed, mlp_gain), norm_full(mixed_far, mlp_gain)], axis=0
    )
    hidden = hidden_of(normed_mlp, gather_half(near, 0), gather_half(far, 0), half)

    if ranks == 2:
        mine = half == rank
        leaving = jnp.dot(
            hidden,
            gather_half(jnp.where(mine, down_far, down_near), 1),
            preferred_element_type=jnp.float32,
        ).astype(jnp.bfloat16)
        got = lax.ppermute(leaving, "tp", SWAP)
        terms = jnp.dot(
            hidden,
            gather_half(jnp.where(mine, down_near, down_far), 1),
            preferred_element_type=jnp.float32,
        ) + got.astype(jnp.float32)
    else:
        low = jnp.where(half == 0, down_near, down_far)
        high = jnp.where(half == 0, down_far, down_near)
        terms = jnp.dot(
            hidden,
            jnp.concatenate([gather_half(low, 1), gather_half(high, 1)], axis=1),
            preferred_element_type=jnp.float32,
        )
        terms = lax.psum_scatter(terms, "tp", scatter_dimension=1, tiled=True)
    back = lax.ppermute(terms[tok_rows:].astype(jnp.bfloat16), "seq", across)
    return (
        mixed.astype(jnp.float32) + (terms[:tok_rows] + back.astype(jnp.float32))
    ).astype(jnp.bfloat16)


def solution(mesh):
    in_specs = (
        P("seq", "tp"),
        P(),
        P(),
        P(None, "tp"),
        P(None, "tp"),
        P(None, "tp"),
        P("tp", None),
        P(),
        P("seq", "tp"),
        P("seq", "tp"),
        P("tp", "seq"),
    )
    out_specs = P("seq", "tp")
    return jax.shard_map(
        per_device, mesh=mesh, in_specs=in_specs, out_specs=out_specs, check_vma=False
    )
```
